256 devices in a mesh: tower: 16 (over z_lo, y, core), dev: 16 (over z_hi, x).
Axes of the slice: x: 4, y: 4, z: 8 (z_hi: 4, z_lo: 2; z = z_hi * 2 + z_lo), core: 2. Of those that a mesh axis runs over, the one named last changes fastest.
Arguments:
- bag_ids: int32 [16, 8192, 32, 4], P('tower', None, 'dev'), may hold values from 0 to 1023
- bag_lengths: int32 [16, 8192, 32], P('tower', None, 'dev'), may hold values from 1 to 4
- tables: bfloat16 [16, 32, 1024, 128], P('tower', 'dev'), may hold values from -3 to 3
- cross_down: bfloat16 [16, 1, 4096, 512], P('tower'), may hold values from -0.09375 to 0.09375
- cross_up: bfloat16 [16, 1, 512, 4096], P('tower'), may hold values from -0.25 to 0.25
- cross_bias: float32 [16, 1, 4096], P('tower'), may hold values from -4 to 4
- proj_weight: bfloat16 [16, 4096, 512], P('tower'), may hold values from -0.09375 to 0.09375
- proj_bias: float32 [16, 512], P('tower'), may hold values from -3 to 3
Outputs:
- interactions: float32 [8192, 120], P(('tower', 'dev'))
The draws below stay inside these ranges and needn't reach their ends.
Inputs may be any that keep to these rules, and one draw needn't show every extreme that they name: `bag_ids`: where table rows travel between devices, each is sent as a whole 32-bit integer, one to a slot; a program may not pack several table rows into one word. `bag_lengths`: where bag lengths travel between devices, a program may pack several of them into one word.
All inputs are finite; a program needn't handle non-finite values.
Results may differ from the reference program's by a relative error of at most 0.0071.
Values may be sent and summed in bfloat16 or wider, within the bound.
A program may use at most 128 MiB of HBM per device.

```python
import jax
import jax.numpy as jnp
import numpy as np
from jax import lax

EMB = 128
FEATS = 32
D = 4096
RANK = 512
OUT = 512
LAYERS = 1
POOL = 4
TROWS = 1024
TOWERS = 16
SAMPLES = 8192


def with_ends(entries, own_key, least, high):
    index_at = [jax.random.randint(jax.random.fold_in(own_key, axis), (), 0, length) for axis, length in enumerate(entries.shape)]
    longest = entries.shape.index(max(entries.shape))
    beside = index_at[:longest] + [(index_at[longest] + 1) % entries.shape[longest]] + index_at[longest + 1:]
    return entries.at[tuple(index_at)].set(least).at[tuple(beside)].set(high)


def steps_of(own_key, dims, shards, smallest, high):
    def one(position, blocks):
        heights = jax.random.uniform(jax.random.fold_in(jax.random.fold_in(own_key, 6), position), (blocks,), jnp.float32, smallest / len(shards), high / len(shards))
        return jnp.repeat(jnp.exp(heights), dims[position] // blocks).reshape((-1,) + (1,) * (len(dims) - position - 1))

    factor_of = one(*shards[0])
    for cut in shards[1:]:
        factor_of = factor_of * one(*cut)
    return factor_of


def noise(stream_key, shape, scale, reach, split=(), kind=jnp.bfloat16):
    entries = scale * jax.random.normal(stream_key, shape, jnp.float32)
    if split:
        entries = entries * steps_of(stream_key, shape, split, -0.22, 0.18)
    return jnp.clip(entries, -reach, reach).astype(kind)


def setup_inputs(seed: int = 0) -> dict:
    streams_of = jax.random.split(jax.random.key(seed), 9)
    return {
        "bag_ids": with_ends(jax.random.randint(streams_of[0], (TOWERS, SAMPLES, FEATS, POOL), 0, TROWS), jax.random.fold_in(streams_of[0], 1), 0, TROWS - 1).astype(jnp.int32),
        "bag_lengths": with_ends(jax.random.randint(streams_of[1], (TOWERS, SAMPLES, FEATS), 1, POOL + 1), jax.random.fold_in(streams_of[1], 1), 1, POOL).astype(jnp.int32),
        "tables": noise(streams_of[2], (TOWERS, FEATS, TROWS, EMB), 0.5, 3.0, ((0, 16), (1, 16))),
        "cross_down": noise(streams_of[3], (TOWERS, LAYERS, D, RANK), D ** -0.5, 0.09375, ((0, 16),)),
        "cross_up": noise(streams_of[4], (TOWERS, LAYERS, RANK, D), RANK ** -0.5, 0.25, ((0, 16),)),
        "cross_bias": noise(streams_of[5], (TOWERS, LAYERS, D), 1.0, 4.0, ((0, 16),), jnp.float32),
        "proj_weight": noise(streams_of[6], (TOWERS, D, OUT), D ** -0.5, 0.09375, ((0, 16),)),
        "proj_bias": noise(streams_of[7], (TOWERS, OUT), 0.5, 3.0, ((0, 16),), jnp.float32),
    }


def pool_rows(tables_one, ids_one, lengths_one):
    total = jnp.zeros(ids_one.shape[:2] + (tables_one.shape[2],), jnp.float32)
    for slot in range(ids_one.shape[2]):
        rows = jax.vmap(lambda table, index: jnp.take(table, index, axis=0), in_axes=(0, 1), out_axes=1)(tables_one, ids_one[:, :, slot])
        live = (slot < lengths_one).astype(jnp.float32)[:, :, None]
        total = total + rows.astype(jnp.float32) * live
    return total.astype(jnp.bfloat16)

def tower_forward(base, down, up, bias, proj, proj_b):
    base_f = base.astype(jnp.float32)
    cross = base
    for layer in range(down.shape[0]):
        low = jnp.dot(cross, down[layer], preferred_element_type=jnp.float32).astype(jnp.bfloat16)
        high = jnp.dot(low, up[layer], preferred_element_type=jnp.float32) + bias[layer]
        cross = (base_f * high + cross.astype(jnp.float32)).astype(jnp.bfloat16)
    return (jnp.dot(cross, proj, preferred_element_type=jnp.float32) + proj_b).astype(jnp.bfloat16)

def one_tower(packed):
    ids_one, lengths_one, tables_one, down, up, bias, proj, proj_b = packed
    pooled = pool_rows(tables_one, ids_one, lengths_one)
    base = pooled.reshape(pooled.shape[0], -1)
    return tower_forward(base, down, up, bias, proj, proj_b)

def reference(bag_ids, bag_lengths, tables, cross_down, cross_up, cross_bias, proj_weight, proj_bias):
    outputs = lax.map(one_tower, (bag_ids, bag_lengths, tables, cross_down, cross_up, cross_bias, proj_weight, proj_bias))
    wide = outputs.astype(jnp.float32)
    gram = jnp.einsum('isk,jsk->sij', wide, wide) / jnp.sqrt(jnp.float32(OUT))
    upper, lower = np.triu_indices(TOWERS, 1)
    return gram[:, upper, lower]
```

```python
import functools

import jax
import jax.numpy as jnp
import numpy as np
from jax import lax
from jax.experimental import pallas as pl
from jax.experimental.pallas import tpu as pltpu
from jax.sharding import PartitionSpec as P

EMB = 128
OUT = 512
MESH = pl.DeviceIdType.MESH
TILE = 256
PROJ_ROWS = 256


def kernel(
    ids_ref,
    len_ref,
    tab_hbm,
    down_hbm,
    up_hbm,
    bias_ref,
    proj_hbm,
    pbias_ref,
    out_ref,
    keys,
    keys_in,
    cols,
    tab,
    sendbuf,
    base,
    down,
    up,
    proj,
    acc,
    low,
    cross,
    outs,
    gath,
    local_sem,
    k_send,
    k_recv,
    t_send,
    t_recv,
    x_send,
    x_recv,
    o_send,
    o_recv,
):
    t = lax.axis_index("tower")
    v = lax.axis_index("dev")
    zh, x = v // 4, v % 4
    right, left, opposite = (zh + 1) % 4, (zh + 3) % 4, (zh + 2) % 4
    zs = (zh, left, right, opposite)

    def on_z(z):
        return (t, z * 4 + x)

    def on_x(step):
        return (t, zh * 4 + (x + step) % 4)

    barrier = pltpu.get_barrier_semaphore()
    for z in (right, left, opposite):
        pl.semaphore_signal(barrier, inc=1, device_id=on_z(z), device_id_type=MESH)
    for step in (1, 2, 3):
        pl.semaphore_signal(barrier, inc=1, device_id=on_x(step), device_id_type=MESH)
    for mask in range(1, 16):
        pl.semaphore_signal(barrier, inc=1, device_id=(t ^ mask, v), device_id_type=MESH)

    own_tab = pltpu.make_async_copy(tab_hbm, tab.at[0], local_sem.at[0])
    own_tab.start()

    slot = lax.broadcasted_iota(jnp.int32, (4, 128), 0)

    def make_keys(b, carry):
        lanes = pl.ds(pl.multiple_of(b * 128, 128), 128)
        halves = []
        for f in range(2):
            row = ids_ref[f, :, lanes]
            live = slot < len_ref[f : f + 1, lanes]
            code = (128 + (row & 127)) << (row >> 7)
            halves.append(jnp.where(live, code, 0))
        keys[b % 4, b // 4] = jnp.concatenate(halves, axis=0)
        return carry

    lax.fori_loop(0, 64, make_keys, 0, unroll=4)

    pl.semaphore_wait(barrier, 21)

    def key_copy(slot_there, z):
        return pltpu.make_async_remote_copy(
            keys.at[z],
            keys_in.at[slot_there - 1],
            k_send.at[slot_there - 1],
            k_recv.at[slot_there - 1],
            device_id=on_z(z),
            device_id_type=MESH,
        )

    key_copies = {1: key_copy(1, right), 2: key_copy(2, left), 3: key_copy(3, opposite)}

    def tab_copy(src, slot_there, f, z):
        return pltpu.make_async_remote_copy(
            src,
            tab.at[slot_there, f],
            t_send.at[slot_there - 1, f],
            t_recv.at[slot_there - 1, f],
            device_id=on_z(z),
            device_id_type=MESH,
        )

    tab_copies = {
        (1, 0): tab_copy(tab_hbm.at[0], 1, 0, right),
        (1, 1): tab_copy(tab_hbm.at[1], 1, 1, right),
        (2, 0): tab_copy(tab_hbm.at[0], 2, 0, left),
        (2, 1): tab_copy(tab_hbm.at[1], 2, 1, left),
        (3, 0): tab_copy(tab.at[1, 0], 3, 0, right),
        (3, 1): tab_copy(tab.at[2, 1], 3, 1, left),
    }
    key_copies[1].start()
    key_copies[2].start()
    tab_copies[1, 0].start()
    tab_copies[2, 1].start()
    key_copies[3].start()
    tab_copies[1, 1].start()
    tab_copies[2, 0].start()

    weights = [
        pltpu.make_async_copy(down_hbm, down, local_sem.at[1]),
        pltpu.make_async_copy(up_hbm, up, local_sem.at[2]),
        pltpu.make_async_copy(proj_hbm, proj, local_sem.at[3]),
    ]

    def turn(rel):
        def one(b, carry):
            block = keys[zh, b] if rel == 0 else keys_in[rel - 1, b]
            turned = block.astype(jnp.float32).T.astype(jnp.bfloat16)
            rows = pl.ds(pl.multiple_of(b * 32, 32), 32)
            for part in range(4):
                cols[rel, part, rows, :] = turned[32 * part : 32 * part + 32]
            return carry

        lax.fori_loop(0, 16, one, 0, unroll=2)

    row_id = lax.broadcasted_iota(jnp.int32, (1, 1024), 1)
    codes = ((128 + (row_id & 127)) << (row_id >> 7)).astype(jnp.float32).astype(jnp.bfloat16)
    one_b, zero_b = jnp.bfloat16(1), jnp.bfloat16(0)

    def tile_of(rel, f, member, r0):
        rows = cols[rel, member, pl.ds(r0, TILE), 4 * f : 4 * f + 4]
        count = None
        for p in range(4):
            hit = jnp.where(rows[:, p : p + 1] == codes, one_b, zero_b)
            count = hit if count is None else count + hit
        summed = jnp.dot(count, tab[rel, f], preferred_element_type=jnp.float32)
        return summed.astype(jnp.bfloat16)

    def columns_of(rel, f):
        return pl.ds(pl.multiple_of(((zs[rel] * 4 + x) * 2 + f) * EMB, EMB), EMB)

    def x_copy(rel, f, step):
        return pltpu.make_async_remote_copy(
            sendbuf.at[step - 1, rel, f],
            base.at[:, columns_of(rel, f)],
            x_send.at[step - 1, rel, f],
            x_recv.at[step - 1, rel, f],
            device_id=on_x(step),
            device_id_type=MESH,
        )

    def pool(rel, f):
        def to_member(i, carry):
            step = lax.select(i == 0, 2, lax.select(i == 1, 1, 3))
            member = (x + step) % 4
            for piece in range(512 // TILE):
                sendbuf[step - 1, rel, f, pl.ds(piece * TILE, TILE)] = tile_of(
                    rel, f, member, piece * TILE
                )
            x_copy(rel, f, step).start()
            return carry

        lax.fori_loop(0, 3, to_member, 0)
        for piece in range(512 // TILE):
            base[pl.ds(piece * TILE, TILE), columns_of(rel, f)] = tile_of(
                rel, f, x, piece * TILE
            )

    def lower(rel, first):
        for f in range(2):
            for step in (1, 2, 3):
                x_copy(rel, f, step).wait_recv()
        part = pl.ds(pl.multiple_of(zs[rel] * 1024, 1024), 1024)
        term = jnp.dot(base[:, part], down[part, :], preferred_element_type=jnp.float32)
        if first:
            acc[...] = term
        else:
            acc[...] += term

    own_tab.wait()
    turn(0)
    pool(0, 0)
    for copy in weights:
        copy.start()
    pool(0, 1)
    for rel in (1, 2):
        key_copies[rel].wait_recv()
        turn(rel)
    tab_copies[1, 0].wait_recv()
    tab_copies[3, 0].start()
    pool(1, 0)
    tab_copies[2, 1].wait_recv()
    tab_copies[3, 1].start()
    pool(2, 1)
    for copy in weights:
        copy.wait()
    lower(0, True)
    key_copies[3].wait_recv()
    turn(3)
    tab_copies[1, 1].wait_recv()
    pool(1, 1)
    tab_copies[2, 0].wait_recv()
    pool(2, 0)
    tab_copies[3, 0].wait_recv()
    pool(3, 0)
    tab_copies[3, 1].wait_recv()
    pool(3, 1)
    lower(1, False)
    lower(2, False)
    lower(3, False)

    low[...] = acc[...].astype(jnp.bfloat16)
    for n in range(16):
        c = slice(256 * n, 256 * n + 256)
        high = jnp.dot(low[...], up[:, c], preferred_element_type=jnp.float32) + bias_ref[:, c]
        b = base[:, c].astype(jnp.float32)
        cross[:, c] = (b * high + b).astype(jnp.bfloat16)

    per = PROJ_ROWS // 32

    def out_copy(mask):
        return pltpu.make_async_remote_copy(
            outs.at[t ^ mask],
            gath.at[t],
            o_send.at[mask],
            o_recv.at[mask],
            device_id=(t ^ mask, v),
            device_id_type=MESH,
        )

    for chunk in range(512 // PROJ_ROWS):
        group = (t // per) ^ chunk
        r0 = pl.multiple_of(group * PROJ_ROWS, PROJ_ROWS)
        value = jnp.dot(
            cross[pl.ds(r0, PROJ_ROWS), :], proj[...], preferred_element_type=jnp.float32
        )
        value = (value + pbias_ref[...]).astype(jnp.bfloat16)
        outs[pl.ds(group * per, per)] = value.reshape(per, 32, OUT)
        for i in range(per):
            mask = chunk * per + i
            if mask:
                out_copy(mask).start()
    gath[t] = outs[t]
    for mask in range(1, 16):
        out_copy(mask).wait_recv()
    out_ref[...] = gath[...]

    for copy in key_copies.values():
        copy.wait_send()
    for copy in tab_copies.values():
        copy.wait_send()
    for rel in range(4):
        for f in range(2):
            for step in (1, 2, 3):
                x_copy(rel, f, step).wait_send()
    for mask in range(1, 16):
        out_copy(mask).wait_send()


def local(bag_ids, bag_lengths, tables, cross_down, cross_up, cross_bias, proj_weight, proj_bias):
    towers = 16
    bf, i32, f32 = jnp.bfloat16, jnp.int32, jnp.float32
    vmem = pl.BlockSpec(memory_space=pltpu.VMEM)
    hbm = pl.BlockSpec(memory_space=pl.ANY)
    dma = pltpu.SemaphoreType.DMA
    gathered = pl.pallas_call(
        kernel,
        out_shape=jax.ShapeDtypeStruct((16, 32, OUT), bf),
        in_specs=[vmem, vmem, hbm, hbm, hbm, vmem, hbm, vmem],
        out_specs=vmem,
        scratch_shapes=[
            pltpu.VMEM((4, 16, 8, 128), i32),
            pltpu.VMEM((3, 16, 8, 128), i32),
            pltpu.VMEM((4, 4, 512, 8), bf),
            pltpu.VMEM((4, 2, 1024, EMB), bf),
            pltpu.VMEM((3, 4, 2, 512, EMB), bf),
            pltpu.VMEM((512, 4096), bf),
            pltpu.VMEM((4096, 512), bf),
            pltpu.VMEM((512, 4096), bf),
            pltpu.VMEM((4096, 512), bf),
            pltpu.VMEM((512, 512), f32),
            pltpu.VMEM((512, 512), bf),
            pltpu.VMEM((512, 4096), bf),
            pltpu.VMEM((16, 32, OUT), bf),
            pltpu.VMEM((16, 32, OUT), bf),
            dma((4,)),
            dma((3,)),
            dma((3,)),
            dma((3, 2)),
            dma((3, 2)),
            dma((3, 4, 2)),
            dma((3, 4, 2)),
            dma((16,)),
            dma((16,)),
        ],
        compiler_params=pltpu.CompilerParams(
            collective_id=0, has_side_effects=True, vmem_limit_bytes=60 << 20
        ),
    )(
        bag_ids[0].transpose(1, 2, 0),
        bag_lengths[0].transpose(1, 0),
        tables[0],
        cross_down[0, 0],
        cross_up[0, 0],
        cross_bias[0],
        proj_weight[0],
        proj_bias,
    )
    gram = jnp.einsum(
        "isk,jsk->sij", gathered, gathered, preferred_element_type=jnp.float32
    ) / jnp.sqrt(jnp.float32(OUT))
    upper, lower = np.triu_indices(towers, 1)
    return gram[:, upper, lower]


def solution(mesh):
    placed = (
        P("tower", None, "dev", None),
        P("tower", None, "dev"),
        P("tower", "dev", None, None),
        P("tower", None, None, None),
        P("tower", None, None, None),
        P("tower", None, None),
        P("tower", None, None),
        P("tower", None),
    )
    return jax.shard_map(
        local, mesh=mesh, in_specs=placed, out_specs=P(("tower", "dev"), None), check_vma=False
    )
```

```python
import functools

import jax
import jax.numpy as jnp
from jax import lax
from jax.experimental import pallas as pl
from jax.experimental.pallas import tpu as pltpu
from jax.sharding import PartitionSpec as P

EMB = 128
OUT = 512
MESH = pl.DeviceIdType.MESH
HALF = 256


def kernel(
    ids_hbm,
    len_hbm,
    tab_hbm,
    down_hbm,
    up_hbm,
    bias_hbm,
    proj_hbm,
    pbias_hbm,
    out_ref,
    ids_ref,
    len_ref,
    bias_ref,
    pbias_ref,
    keys,
    keys_in,
    cols,
    tab,
    sendbuf,
    base,
    down,
    up,
    proj,
    acc,
    low,
    cross,
    outs,
    gath,
    local_sem,
    k_send,
    k_recv,
    t_send,
    t_recv,
    f_send,
    f_recv,
    x_send,
    x_recv,
    o_send,
    o_recv,
):
    t = lax.axis_index("tower")
    v = lax.axis_index("dev")
    zh, x = v // 4, v % 4
    core, place = t % 2, t // 2
    right, left, opposite = (zh + 1) % 4, (zh + 3) % 4, (zh + 2) % 4
    zs = (zh, left, right, opposite)

    def on_z(z):
        return (t, z * 4 + x)

    def on_x(step):
        return (t, zh * 4 + (x + step) % 4)

    def half_of(chunk):
        return (core + chunk) % 2

    def rows_of(chunk):
        return pl.ds(pl.multiple_of(half_of(chunk) * HALF, HALF), HALF)

    barrier = pltpu.get_barrier_semaphore()
    for z in (right, left, opposite):
        pl.semaphore_signal(barrier, inc=1, device_id=on_z(z), device_id_type=MESH)
    for step in (1, 2, 3):
        pl.semaphore_signal(barrier, inc=1, device_id=on_x(step), device_id_type=MESH)
    for mask in range(1, 16):
        pl.semaphore_signal(barrier, inc=1, device_id=(t ^ mask, v), device_id_type=MESH)

    def fetch(k, src, dst):
        return pltpu.make_async_copy(src, dst, local_sem.at[k])

    first = [fetch(0, ids_hbm, ids_ref), fetch(1, len_hbm, len_ref)]
    own_tab = fetch(2, tab_hbm, tab.at[0])
    weights = [
        fetch(3, down_hbm, down),
        fetch(4, up_hbm, up),
        fetch(5, proj_hbm, proj),
        fetch(6, bias_hbm, bias_ref),
        fetch(7, pbias_hbm, pbias_ref),
    ]
    for copy in first:
        copy.start()
    own_tab.start()
    for copy in first:
        copy.wait()

    slot = lax.broadcasted_iota(jnp.int32, (4, 128), 0)

    def make_keys(b, carry):
        z, pair = b % 4, b // 4
        for f in range(2):
            halves = []
            for odd in range(2):
                start = (pair * 2 + odd) * 512 + z * 128
                lanes = pl.ds(pl.multiple_of(start, 128), 128)
                row = ids_ref[f, :, lanes]
                live = slot < len_ref[f : f + 1, lanes]
                code = (128 + (row & 127)) << (row >> 7)
                halves.append(jnp.where(live, code, 0))
            keys[z, f, pair] = jnp.concatenate(halves, axis=0)
        return carry

    lax.fori_loop(0, 32, make_keys, 0, unroll=2)

    def key_copy(there, f):
        z = (None, right, left, opposite)[there]
        return pltpu.make_async_remote_copy(
            keys.at[z, f],
            keys_in.at[there - 1, f],
            k_send.at[there - 1, f],
            k_recv.at[there - 1, f],
            device_id=on_z(z),
            device_id_type=MESH,
        )

    def tab_copy(there, f):
        return pltpu.make_async_remote_copy(
            tab_hbm.at[f],
            tab.at[there, f],
            t_send.at[there - 1, f],
            t_recv.at[there - 1, f],
            device_id=on_z((None, right, left)[there]),
            device_id_type=MESH,
        )

    def forward(there, f):
        rows = pl.ds((there - 1) * 512, 512)
        return pltpu.make_async_remote_copy(
            tab.at[there, f, rows],
            tab.at[3, f, rows],
            f_send.at[there - 1, f],
            f_recv.at[there - 1, f],
            device_id=on_z((None, right, left)[there]),
            device_id_type=MESH,
        )

    def turn(rel, f):
        def one(b, carry):
            block = keys[zh, f, b] if rel == 0 else keys_in[rel - 1, f, b]
            turned = block.astype(jnp.float32).T.astype(jnp.bfloat16)
            rows = pl.ds(pl.multiple_of(b * 32, 32), 32)
            for part in range(4):
                for odd in range(2):
                    cols[rel, f, part, odd, rows, :] = turned[
                        32 * part : 32 * part + 32, 4 * odd : 4 * odd + 4
                    ]
            return carry

        lax.fori_loop(0, 8, one, 0, unroll=2)

    row_id = lax.broadcasted_iota(jnp.int32, (1, 1024), 1)
    codes = ((128 + (row_id & 127)) << (row_id >> 7)).astype(jnp.float32).astype(jnp.bfloat16)
    one_b, zero_b = jnp.bfloat16(1), jnp.bfloat16(0)

    def tile_of(rel, f, member, half):
        rows = cols[rel, f, member, half]
        count = None
        for p in range(4):
            hit = jnp.where(rows[:, p : p + 1] == codes, one_b, zero_b)
            count = hit if count is None else count + hit
        summed = jnp.dot(count, tab[rel, f], preferred_element_type=jnp.float32)
        return summed.astype(jnp.bfloat16)

    def columns_of(rel, f):
        return pl.ds(pl.multiple_of(((zs[rel] * 4 + x) * 2 + f) * EMB, EMB), EMB)

    def x_copy(rel, f, chunk, step):
        return pltpu.make_async_remote_copy(
            sendbuf.at[step - 1, rel, f, chunk],
            base.at[rows_of(chunk), columns_of(rel, f)],
            x_send.at[step - 1, rel, f, chunk],
            x_recv.at[step - 1, rel, f, chunk],
            device_id=on_x(step),
            device_id_type=MESH,
        )

    def pool(rel, f, chunks=(0, 1), send=True):
        def to_member(i, carry):
            place_in, chunk = i % 3, chunks[0] + i // 3
            step = lax.select(place_in == 0, 2, lax.select(place_in == 1, 1, 3))
            sendbuf[step - 1, rel, f, chunk] = tile_of(rel, f, (x + step) % 4, half_of(chunk))
            if send:
                x_copy(rel, f, chunk, step).start()
            return carry

        lax.fori_loop(0, 3 * len(chunks), to_member, 0)

        def to_self(i, carry):
            chunk = chunks[0] + i
            base[rows_of(chunk), columns_of(rel, f)] = tile_of(rel, f, x, half_of(chunk))
            return carry

        lax.fori_loop(0, len(chunks), to_self, 0)

    def part_of(rel):
        return pl.ds(pl.multiple_of(zs[rel] * 1024, 1024), 1024)

    def arrived(rel, chunk):
        for f in range(2):
            for step in (1, 2, 3):
                x_copy(rel, f, chunk, step).wait_recv()

    def lower(rel):
        arrived(rel, 0)
        arrived(rel, 1)
        part = part_of(rel)
        term = jnp.dot(base[:, part], down[part, :], preferred_element_type=jnp.float32)
        if rel == 0:
            acc[...] = term
        else:
            acc[...] += term

    turn(0, 0)
    own_tab.wait()
    pool(0, 0, send=False)
    pl.semaphore_wait(barrier, 21)
    for there in (1, 2):
        key_copy(there, 0).start()
        tab_copy(there, 0).start()
    for chunk in range(2):
        for step in (2, 1, 3):
            x_copy(0, 0, chunk, step).start()
    for there in (1, 2, 3):
        key_copy(there, 1).start()
    key_copy(3, 0).start()
    for there in (1, 2):
        tab_copy(there, 1).start()
    turn(0, 1)
    pool(0, 1)
    for copy in weights:
        copy.start()
    for f in range(2):
        for rel in (1, 2):
            key_copy(rel, f).wait_recv()
            turn(rel, f)
        for rel in (1, 2):
            tab_copy(rel, f).wait_recv()
            forward(rel, f).start()
        for rel in (1, 2):
            pool(rel, f)
        if f == 0:
            for copy in weights:
                copy.wait()
            lower(0)
    for f in range(2):
        key_copy(3, f).wait_recv()
        turn(3, f)
    for f in range(2):
        for there in (1, 2):
            forward(there, f).wait_recv()
        pool(3, f, (0,))
    for f in range(2):
        pool(3, f, (1,))
    lower(1)
    lower(2)

    def out_copy(mask):
        return pltpu.make_async_remote_copy(
            outs.at[t ^ mask],
            gath.at[t],
            o_send.at[mask],
            o_recv.at[mask],
            device_id=(t ^ mask, v),
            device_id_type=MESH,
        )

    for chunk in range(2):
        r = rows_of(chunk)
        arrived(3, chunk)
        part = part_of(3)
        total = acc[r, :] + jnp.dot(
            base[r, part], down[part, :], preferred_element_type=jnp.float32
        )
        low[...] = total.astype(jnp.bfloat16)
        for n in range(16):
            c = slice(256 * n, 256 * n + 256)
            high = jnp.dot(low[...], up[:, c], preferred_element_type=jnp.float32) + bias_ref[:, c]
            b = base[r, c].astype(jnp.float32)
            cross[:, c] = (b * high + b).astype(jnp.bfloat16)
        value = jnp.dot(cross[...], proj[...], preferred_element_type=jnp.float32)
        value = (value + pbias_ref[...]).astype(jnp.bfloat16).reshape(8, 32, OUT)
        for i in range(8):
            outs[2 * i + half_of(chunk)] = value[i]
        for i in range(8):
            mask = 2 * i + chunk
            if mask:
                out_copy(mask).start()
    gath[t] = outs[t]
    for mask in range(1, 16):
        out_copy(mask).wait_recv()

    full = gath[...].reshape(512, OUT)
    gram = lax.dot_general(
        full, full, (((1,), (1,)), ((), ())), preferred_element_type=jnp.float32
    )
    same = (
        lax.broadcasted_iota(jnp.int32, (512, 512), 0) % 32
        == lax.broadcasted_iota(jnp.int32, (512, 512), 1) % 32
    )
    gram = jnp.where(same, gram, 0.0)
    fold = (
        lax.broadcasted_iota(jnp.int32, (512, 128), 0) // 32
        == lax.broadcasted_iota(jnp.int32, (512, 128), 1)
    ).astype(jnp.float32).astype(jnp.bfloat16)
    hi = gram.astype(jnp.bfloat16)
    rest = gram - hi.astype(jnp.float32)
    mid = rest.astype(jnp.bfloat16)
    lo = (rest - mid.astype(jnp.float32)).astype(jnp.bfloat16)
    folded = sum(jnp.dot(p, fold, preferred_element_type=jnp.float32) for p in (lo, mid, hi))
    lane = lax.broadcasted_iota(jnp.int32, (32, 128), 1)
    result = jnp.zeros((32, 128), jnp.float32)
    start = 0
    for i in range(15):
        moved = pltpu.roll(folded[32 * i : 32 * i + 32], (start - i - 1) % 128, 1)
        result = jnp.where((lane >= start) & (lane < start + 15 - i), moved, result)
        start += 15 - i
    out_ref[...] = (result / jnp.sqrt(jnp.float32(OUT)))[:, :120]

    for f in range(2):
        for there in (1, 2, 3):
            key_copy(there, f).wait_send()
        for there in (1, 2):
            tab_copy(there, f).wait_send()
            forward(there, f).wait_send()
    for rel in range(4):
        for f in range(2):
            for chunk in range(2):
                for step in (1, 2, 3):
                    x_copy(rel, f, chunk, step).wait_send()
    for mask in range(1, 16):
        out_copy(mask).wait_send()


def local(bag_ids, bag_lengths, tables, cross_down, cross_up, cross_bias, proj_weight, proj_bias):
    bf, i32, f32 = jnp.bfloat16, jnp.int32, jnp.float32
    hbm = pl.BlockSpec(memory_space=pl.ANY)
    dma = pltpu.SemaphoreType.DMA
    return pl.pallas_call(
        kernel,
        out_shape=jax.ShapeDtypeStruct((32, 120), f32),
        in_specs=[hbm] * 8,
        out_specs=pl.BlockSpec(memory_space=pltpu.VMEM),
        scratch_shapes=[
            pltpu.VMEM((2, 4, 8192), i32),
            pltpu.VMEM((2, 8192), i32),
            pltpu.VMEM((1, 4096), f32),
            pltpu.VMEM((1, OUT), f32),
            pltpu.VMEM((4, 2, 8, 8, 128), i32),
            pltpu.VMEM((3, 2, 8, 8, 128), i32),
            pltpu.VMEM((4, 2, 4, 2, HALF, 4), bf),
            pltpu.VMEM((4, 2, 1024, EMB), bf),
            pltpu.VMEM((3, 4, 2, 2, HALF, EMB), bf),
            pltpu.VMEM((512, 4096), bf),
            pltpu.VMEM((4096, 512), bf),
            pltpu.VMEM((512, 4096), bf),
            pltpu.VMEM((4096, 512), bf),
            pltpu.VMEM((512, 512), f32),
            pltpu.VMEM((HALF, 512), bf),
            pltpu.VMEM((HALF, 4096), bf),
            pltpu.VMEM((16, 32, OUT), bf),
            pltpu.VMEM((16, 32, OUT), bf),
            dma((8,)),
            dma((3, 2)),
            dma((3, 2)),
            dma((2, 2)),
            dma((2, 2)),
            dma((2, 2)),
            dma((2, 2)),
            dma((3, 4, 2, 2)),
            dma((3, 4, 2, 2)),
            dma((16,)),
            dma((16,)),
        ],
        compiler_params=pltpu.CompilerParams(
            collective_id=0, has_side_effects=True, vmem_limit_bytes=60 << 20
        ),
    )(
        bag_ids[0].transpose(1, 2, 0),
        bag_lengths[0].transpose(1, 0),
        tables[0],
        cross_down[0, 0],
        cross_up[0, 0],
        cross_bias[0],
        proj_weight[0],
        proj_bias,
    )


def solution(mesh):
    placed = (
        P("tower", None, "dev", None),
        P("tower", None, "dev"),
        P("tower", "dev", None, None),
        P("tower", None, None, None),
        P("tower", None, None, None),
        P("tower", None, None),
        P("tower", None, None),
        P("tower", None),
    )
    return jax.shard_map(
        local, mesh=mesh, in_specs=placed, out_specs=P(("tower", "dev"), None), check_vma=False
    )
```

```python
import functools

import jax
import jax.numpy as jnp
from jax import lax
from jax.experimental import pallas as pl
from jax.experimental.pallas import tpu as pltpu
from jax.sharding import PartitionSpec as P

EMB = 128
OUT = 512
MESH = pl.DeviceIdType.MESH
HALF = 256


def kernel(
    ids_hbm,
    len_hbm,
    tab_hbm,
    down_hbm,
    up_hbm,
    bias_hbm,
    proj_hbm,
    pbias_hbm,
    out_ref,
    ids_ref,
    len_ref,
    bias_ref,
    pbias_ref,
    keys,
    keys_in,
    codes,
    turned,
    tab,
    sendbuf,
    base,
    down,
    up,
    proj,
    acc,
    low,
    cross,
    outs,
    gath,
    local_sem,
    k_send,
    k_recv,
    t_send,
    t_recv,
    f_send,
    f_recv,
    own_sem,
    pace,
    x_send,
    x_recv,
    o_send,
    o_recv,
):
    t = lax.axis_index("tower")
    v = lax.axis_index("dev")
    zh, x = v // 4, v % 4
    core, place = t % 2, t // 2
    right, left, opposite = (zh + 1) % 4, (zh + 3) % 4, (zh + 2) % 4
    zs = (zh, left, right, opposite)

    def on_z(z):
        return (t, z * 4 + x)

    def on_x(step):
        return (t, zh * 4 + (x + step) % 4)

    def half_of(chunk):
        return (core + chunk) % 2

    def rows_of(chunk):
        return pl.ds(pl.multiple_of(half_of(chunk) * HALF, HALF), HALF)

    barrier = pltpu.get_barrier_semaphore()
    for z in (right, left, opposite):
        pl.semaphore_signal(barrier, inc=1, device_id=on_z(z), device_id_type=MESH)
    for step in (1, 2, 3):
        pl.semaphore_signal(barrier, inc=1, device_id=on_x(step), device_id_type=MESH)
    for mask in range(1, 16):
        pl.semaphore_signal(barrier, inc=1, device_id=(t ^ mask, v), device_id_type=MESH)

    def fetch(k, src, dst):
        return pltpu.make_async_copy(src, dst, local_sem.at[k])

    first = [fetch(0, ids_hbm, ids_ref), fetch(1, len_hbm, len_ref)]
    own_tab = fetch(2, tab_hbm, tab.at[0])
    weights = [
        fetch(3, down_hbm, down),
        fetch(4, up_hbm, up),
        fetch(5, proj_hbm, proj),
        fetch(6, bias_hbm, bias_ref),
        fetch(7, pbias_hbm, pbias_ref),
    ]
    for copy in first:
        copy.start()
    own_tab.start()
    for copy in first:
        copy.wait()

    slot = lax.broadcasted_iota(jnp.int32, (4, 128), 0)

    def make_keys(n, carry):
        z, half, b = n % 4, (n // 4) % 2, n // 8
        for f in range(2):
            groups = []
            for o in range(2):
                start = (4 * b + 2 * o + half) * 512 + z * 128
                lanes = pl.ds(pl.multiple_of(start, 128), 128)
                row = ids_ref[f, :, lanes]
                live = slot < len_ref[f : f + 1, lanes]
                code = (128 + (row & 127)) << (row >> 7)
                groups.append(jnp.where(live, code, 0))
            keys[z, f, half, b] = jnp.concatenate(groups, axis=0)
        return carry

    lax.fori_loop(0, 32, make_keys, 0, unroll=2)

    def key_copy(there, f):
        z = (None, right, left, opposite)[there]
        return pltpu.make_async_remote_copy(
            keys.at[z, f],
            keys_in.at[there - 1, f],
            k_send.at[there - 1, f],
            k_recv.at[there - 1, f],
            device_id=on_z(z),
            device_id_type=MESH,
        )

    def tab_copy(there, f):
        return pltpu.make_async_remote_copy(
            tab_hbm.at[f],
            tab.at[there, f],
            t_send.at[there - 1, f],
            t_recv.at[there - 1, f],
            device_id=on_z((None, right, left)[there]),
            device_id_type=MESH,
        )

    def forward(there, f):
        rows = pl.ds((there - 1) * 512, 512)
        return pltpu.make_async_remote_copy(
            tab.at[there, f, rows],
            tab.at[3, f, rows],
            f_send.at[there - 1, f],
            f_recv.at[there - 1, f],
            device_id=on_z((None, right, left)[there]),
            device_id_type=MESH,
        )

    row_id = lax.broadcasted_iota(jnp.int32, (1024, 128), 0)
    codes[...] = ((128 + (row_id & 127)) << (row_id >> 7)).astype(jnp.float32).astype(jnp.bfloat16)
    lane_of = lax.broadcasted_iota(jnp.int32, (8, 128), 0) % 4

    def turn(rel, f):
        turned[f] = tab[rel, f].astype(jnp.float32).T.astype(jnp.bfloat16)

    def tile(rel, f, chunk, b):
        half = half_of(chunk)
        key = keys[zh, f, half, b] if rel == 0 else keys_in[rel - 1, f, half, b]
        key = key.astype(jnp.float32)
        weight = jnp.ones((8, 128), jnp.float32)
        for r in (1, 2, 3):
            other = jnp.where(lane_of >= r, pltpu.roll(key, r, 0), pltpu.roll(key, r + 4, 0))
            weight = weight + jnp.where(other == key, 1.0, 0.0)
        counts = []
        for o in range(2):
            count = jnp.zeros((1024, 128), jnp.bfloat16)
            for p in range(4 * o, 4 * o + 4):
                k, w = (
                    jnp.tile(jnp.broadcast_to(a[p : p + 1], (16, 128)).astype(jnp.bfloat16), (64, 1))
                    for a in (key, weight)
                )
                count = jnp.where(k == codes[...], w, count)
            counts.append(count)
        pooled = jnp.dot(
            turned[f], jnp.concatenate(counts, axis=1), preferred_element_type=jnp.float32
        )
        for o in range(2):
            block = pooled[:, 128 * o : 128 * o + 128].T.astype(jnp.bfloat16)
            rows = pl.ds(pl.multiple_of((2 * b + o) * 32, 32), 32)
            for member in range(4):
                step = (member - x + 4) % 4
                sendbuf[step, rel, f, chunk, rows, :] = block[32 * member : 32 * member + 32]

    def columns_of(rel, f):
        return pl.ds(pl.multiple_of(((zs[rel] * 4 + x) * 2 + f) * EMB, EMB), EMB)

    def x_copy(rel, f, chunk, step):
        return pltpu.make_async_remote_copy(
            sendbuf.at[step, rel, f, chunk],
            base.at[rows_of(chunk), columns_of(rel, f)],
            x_send.at[step - 1, rel, f, chunk],
            x_recv.at[step - 1, rel, f, chunk],
            device_id=on_x(step),
            device_id_type=MESH,
        )

    def own_copy(rel, f, chunk):
        return pltpu.make_async_copy(
            sendbuf.at[0, rel, f, chunk],
            base.at[rows_of(chunk), columns_of(rel, f)],
            own_sem.at[rel, f, chunk],
        )

    def fill(rel, f, chunk):
        def one(b, carry):
            tile(rel, f, chunk, b)
            return carry

        lax.fori_loop(0, 4, one, 0)

    def give(rel, f, chunk):
        for step in (2, 1, 3):
            x_copy(rel, f, chunk, step).start()
        own_copy(rel, f, chunk).start()

    def pool(rel, f):
        turn(rel, f)
        for chunk in range(2):
            fill(rel, f, chunk)
            give(rel, f, chunk)

    def tell(stage):
        pl.semaphore_signal(pace.at[stage], inc=1, device_id=(t ^ 8, v), device_id_type=MESH)

    def hear(stage):
        pl.semaphore_wait(pace.at[stage], 1)

    def part_of(rel):
        return pl.ds(pl.multiple_of(zs[rel] * 1024, 1024), 1024)

    def arrived(rel, chunk):
        for f in range(2):
            for step in (1, 2, 3):
                x_copy(rel, f, chunk, step).wait_recv()
            own_copy(rel, f, chunk).wait()

    def lower(rel):
        arrived(rel, 0)
        arrived(rel, 1)
        part = part_of(rel)
        term = jnp.dot(base[:, part], down[part, :], preferred_element_type=jnp.float32)
        if rel == 0:
            acc[...] = term
        else:
            acc[...] += term

    own_tab.wait()
    turn(0, 0)
    fill(0, 0, 0)
    fill(0, 0, 1)
    pl.semaphore_wait(barrier, 21)
    for there in (1, 2):
        key_copy(there, 0).start()
        tab_copy(there, 0).start()
    give(0, 0, 0)
    give(0, 0, 1)
    pool(0, 1)
    for copy in weights:
        copy.start()
    for there in (1, 2):
        key_copy(there, 1).start()
    for f in range(2):
        key_copy(3, f).start()
    for there in (1, 2):
        tab_copy(there, 0).wait_send()
    tell(0)
    for rel in (1, 2):
        key_copy(rel, 0).wait_recv()
        tab_copy(rel, 0).wait_recv()
        pool(rel, 0)
        if rel == 1:
            hear(0)
            for there in (1, 2):
                tab_copy(there, 1).start()
    for copy in weights:
        copy.wait()
    lower(0)
    for there in (1, 2):
        tab_copy(there, 1).wait_send()
    tell(1)
    for rel in (1, 2):
        key_copy(rel, 1).wait_recv()
        tab_copy(rel, 1).wait_recv()
        pool(rel, 1)
        if rel == 1:
            hear(1)
            for there in (1, 2):
                forward(there, 0).start()
    for there in (1, 2):
        forward(there, 0).wait_send()
        forward(there, 1).start()
    for f in range(2):
        key_copy(3, f).wait_recv()
        for there in (1, 2):
            forward(there, f).wait_recv()
        turn(3, f)
        fill(3, f, 0)
        give(3, f, 0)
        fill(3, f, 1)
    lower(1)
    lower(2)
    for f in range(2):
        for step in (1, 2, 3):
            x_copy(3, f, 0, step).wait_send()
    for f in range(2):
        give(3, f, 1)

    def out_copy(mask):
        return pltpu.make_async_remote_copy(
            outs.at[t ^ mask],
            gath.at[t],
            o_send.at[mask],
            o_recv.at[mask],
            device_id=(t ^ mask, v),
            device_id_type=MESH,
        )

    for chunk in range(2):
        r = rows_of(chunk)
        arrived(3, chunk)
        part = part_of(3)
        total = acc[r, :] + jnp.dot(
            base[r, part], down[part, :], preferred_element_type=jnp.float32
        )
        low[...] = total.astype(jnp.bfloat16)
        for n in range(16):
            c = slice(256 * n, 256 * n + 256)
            high = jnp.dot(low[...], up[:, c], preferred_element_type=jnp.float32) + bias_ref[:, c]
            b = base[r, c].astype(jnp.float32)
            cross[:, c] = (b * high + b).astype(jnp.bfloat16)
        value = jnp.dot(cross[...], proj[...], preferred_element_type=jnp.float32)
        value = (value + pbias_ref[...]).astype(jnp.bfloat16).reshape(8, 32, OUT)
        for i in range(8):
            outs[2 * i + half_of(chunk)] = value[i]
        for i in range(8):
            mask = 2 * i + chunk
            if mask:
                out_copy(mask).start()
    gath[t] = outs[t]
    for mask in range(1, 16):
        out_copy(mask).wait_recv()

    full = gath[...].reshape(512, OUT)
    gram = lax.dot_general(
        full, full, (((1,), (1,)), ((), ())), preferred_element_type=jnp.float32
    )
    same = (
        lax.broadcasted_iota(jnp.int32, (512, 512), 0) % 32
        == lax.broadcasted_iota(jnp.int32, (512, 512), 1) % 32
    )
    gram = jnp.where(same, gram, 0.0)
    fold = (
        lax.broadcasted_iota(jnp.int32, (512, 128), 0) // 32
        == lax.broadcasted_iota(jnp.int32, (512, 128), 1)
    ).astype(jnp.float32).astype(jnp.bfloat16)
    hi = gram.astype(jnp.bfloat16)
    rest = gram - hi.astype(jnp.float32)
    mid = rest.astype(jnp.bfloat16)
    lo = (rest - mid.astype(jnp.float32)).astype(jnp.bfloat16)
    folded = sum(jnp.dot(p, fold, preferred_element_type=jnp.float32) for p in (lo, mid, hi))
    lane = lax.broadcasted_iota(jnp.int32, (32, 128), 1)
    result = jnp.zeros((32, 128), jnp.float32)
    start = 0
    for i in range(15):
        moved = pltpu.roll(folded[32 * i : 32 * i + 32], (start - i - 1) % 128, 1)
        result = jnp.where((lane >= start) & (lane < start + 15 - i), moved, result)
        start += 15 - i
    out_ref[...] = (result / jnp.sqrt(jnp.float32(OUT)))[:, :120]

    for f in range(2):
        for there in (1, 2, 3):
            key_copy(there, f).wait_send()
    for there in (1, 2):
        forward(there, 1).wait_send()
    for rel in range(4):
        for f in range(2):
            for chunk in range(2):
                if (rel, chunk) != (3, 0):
                    for step in (1, 2, 3):
                        x_copy(rel, f, chunk, step).wait_send()
    for mask in range(1, 16):
        out_copy(mask).wait_send()


def local(bag_ids, bag_lengths, tables, cross_down, cross_up, cross_bias, proj_weight, proj_bias):
    bf, i32, f32 = jnp.bfloat16, jnp.int32, jnp.float32
    hbm = pl.BlockSpec(memory_space=pl.ANY)
    dma = pltpu.SemaphoreType.DMA
    return pl.pallas_call(
        kernel,
        out_shape=jax.ShapeDtypeStruct((32, 120), f32),
        in_specs=[hbm] * 8,
        out_specs=pl.BlockSpec(memory_space=pltpu.VMEM),
        scratch_shapes=[
            pltpu.VMEM((2, 4, 8192), i32),
            pltpu.VMEM((2, 8192), i32),
            pltpu.VMEM((1, 4096), f32),
            pltpu.VMEM((1, OUT), f32),
            pltpu.VMEM((4, 2, 2, 4, 8, 128), i32),
            pltpu.VMEM((3, 2, 2, 4, 8, 128), i32),
            pltpu.VMEM((1024, 128), bf),
            pltpu.VMEM((2, EMB, 1024), bf),
            pltpu.VMEM((4, 2, 1024, EMB), bf),
            pltpu.VMEM((4, 4, 2, 2, HALF, EMB), bf),
            pltpu.VMEM((512, 4096), bf),
            pltpu.VMEM((4096, 512), bf),
            pltpu.VMEM((512, 4096), bf),
            pltpu.VMEM((4096, 512), bf),
            pltpu.VMEM((512, 512), f32),
            pltpu.VMEM((HALF, 512), bf),
            pltpu.VMEM((HALF, 4096), bf),
            pltpu.VMEM((16, 32, OUT), bf),
            pltpu.VMEM((16, 32, OUT), bf),
            dma((8,)),
            dma((3, 2)),
            dma((3, 2)),
            dma((2, 2)),
            dma((2, 2)),
            dma((2, 2)),
            dma((2, 2)),
            dma((4, 2, 2)),
            pltpu.SemaphoreType.REGULAR((2,)),
            dma((3, 4, 2, 2)),
            dma((3, 4, 2, 2)),
            dma((16,)),
            dma((16,)),
        ],
        compiler_params=pltpu.CompilerParams(
            collective_id=0, has_side_effects=True, vmem_limit_bytes=60 << 20
        ),
    )(
        bag_ids[0].transpose(1, 2, 0),
        bag_lengths[0].transpose(1, 0),
        tables[0],
        cross_down[0, 0],
        cross_up[0, 0],
        cross_bias[0],
        proj_weight[0],
        proj_bias,
    )


def solution(mesh):
    placed = (
        P("tower", None, "dev", None),
        P("tower", None, "dev"),
        P("tower", "dev", None, None),
        P("tower", None, None, None),
        P("tower", None, None, None),
        P("tower", None, None),
        P("tower", None, None),
        P("tower", None),
    )
    return jax.shard_map(
        local, mesh=mesh, in_specs=placed, out_specs=P(("tower", "dev"), None), check_vma=False
    )
```

```python
import functools

import jax
import jax.numpy as jnp
from jax import lax
from jax.experimental import pallas as pl
from jax.experimental.pallas import tpu as pltpu
from jax.sharding import PartitionSpec as P

EMB = 128
OUT = 512
MESH = pl.DeviceIdType.MESH
HALF = 256


def kernel(
    ids_hbm,
    len_hbm,
    tab_hbm,
    down_hbm,
    up_hbm,
    bias_hbm,
    proj_hbm,
    pbias_hbm,
    out_ref,
    ids_ref,
    len_ref,
    bias_ref,
    pbias_ref,
    keys,
    keys_in,
    codes,
    turned,
    tab,
    sendbuf,
    base,
    down,
    up,
    proj,
    acc,
    low,
    cross,
    outs,
    gath,
    local_sem,
    k_send,
    k_recv,
    t_send,
    t_recv,
    f_send,
    f_recv,
    own_sem,
    pace,
    x_send,
    x_recv,
    o_send,
    o_recv,
):
    t = lax.axis_index("tower")
    v = lax.axis_index("dev")
    zh, x = v // 4, v % 4
    core, place = t % 2, t // 2
    right, left, opposite = (zh + 1) % 4, (zh + 3) % 4, (zh + 2) % 4
    zs = (zh, left, right, opposite)

    def on_z(z):
        return (t, z * 4 + x)

    def on_x(step):
        return (t, zh * 4 + (x + step) % 4)

    def half_of(chunk):
        return (core + chunk) % 2

    def rows_of(chunk):
        return pl.ds(pl.multiple_of(half_of(chunk) * HALF, HALF), HALF)

    barrier = pltpu.get_barrier_semaphore()
    for z in (right, left, opposite):
        pl.semaphore_signal(barrier, inc=1, device_id=on_z(z), device_id_type=MESH)
    for step in (1, 2, 3):
        pl.semaphore_signal(barrier, inc=1, device_id=on_x(step), device_id_type=MESH)
    for mask in range(1, 16):
        pl.semaphore_signal(barrier, inc=1, device_id=(t ^ mask, v), device_id_type=MESH)

    def fetch(k, src, dst):
        return pltpu.make_async_copy(src, dst, local_sem.at[k])

    first = [fetch(0, ids_hbm, ids_ref), fetch(1, len_hbm, len_ref)]
    own_tab = fetch(2, tab_hbm, tab.at[0])
    weights = [
        fetch(3, down_hbm, down),
        fetch(4, up_hbm, up),
        fetch(5, proj_hbm, proj),
        fetch(6, bias_hbm, bias_ref),
        fetch(7, pbias_hbm, pbias_ref),
    ]
    for copy in first:
        copy.start()
    own_tab.start()
    for copy in first:
        copy.wait()

    slot = lax.broadcasted_iota(jnp.int32, (4, 128), 0)

    def make_keys(n, carry):
        z, half, b = n % 4, (n // 4) % 2, n // 8
        for f in range(2):
            groups = []
            for o in range(2):
                start = (4 * b + 2 * o + half) * 512 + z * 128
                lanes = pl.ds(pl.multiple_of(start, 128), 128)
                row = ids_ref[f, :, lanes]
                live = slot < len_ref[f : f + 1, lanes]
                code = (128 + (row & 127)) << (row >> 7)
                groups.append(jnp.where(live, code, 0))
            keys[z, f, half, b] = jnp.concatenate(groups, axis=0)
        return carry

    lax.fori_loop(0, 32, make_keys, 0, unroll=2)

    def key_copy(there, f):
        z = (None, right, left, opposite)[there]
        return pltpu.make_async_remote_copy(
            keys.at[z, f],
            keys_in.at[there - 1, f],
            k_send.at[there - 1, f],
            k_recv.at[there - 1, f],
            device_id=on_z(z),
            device_id_type=MESH,
        )

    def tab_copy(there, f):
        return pltpu.make_async_remote_copy(
            tab_hbm.at[f],
            tab.at[there, f],
            t_send.at[there - 1, f],
            t_recv.at[there - 1, f],
            device_id=on_z((None, right, left)[there]),
            device_id_type=MESH,
        )

    def forward(there, f):
        rows = pl.ds((there - 1) * 512, 512)
        return pltpu.make_async_remote_copy(
            tab.at[there, f, rows],
            tab.at[3, f, rows],
            f_send.at[there - 1, f],
            f_recv.at[there - 1, f],
            device_id=on_z((None, right, left)[there]),
            device_id_type=MESH,
        )

    row_id = lax.broadcasted_iota(jnp.int32, (1024, 128), 0)
    codes[...] = ((128 + (row_id & 127)) << (row_id >> 7)).astype(jnp.float32).astype(jnp.bfloat16)
    lane_of = lax.broadcasted_iota(jnp.int32, (8, 128), 0) % 4

    def turn(rel, f):
        turned[f] = tab[rel, f].astype(jnp.float32).T.astype(jnp.bfloat16)

    def tile(rel, f, chunk, b):
        half = half_of(chunk)
        key = keys[zh, f, half, b] if rel == 0 else keys_in[rel - 1, f, half, b]
        key = key.astype(jnp.float32)
        weight = jnp.ones((8, 128), jnp.float32)
        for r in (1, 2, 3):
            other = jnp.where(lane_of >= r, pltpu.roll(key, r, 0), pltpu.roll(key, r + 4, 0))
            weight = weight + jnp.where(other == key, 1.0, 0.0)
        counts = []
        for o in range(2):
            count = jnp.zeros((1024, 128), jnp.bfloat16)
            for p in range(4 * o, 4 * o + 4):
                k, w = (
                    jnp.tile(jnp.broadcast_to(a[p : p + 1], (16, 128)).astype(jnp.bfloat16), (64, 1))
                    for a in (key, weight)
                )
                count = jnp.where(k == codes[...], w, count)
            counts.append(count)
        pooled = jnp.dot(
            turned[f], jnp.concatenate(counts, axis=1), preferred_element_type=jnp.float32
        )
        for o in range(2):
            block = pooled[:, 128 * o : 128 * o + 128].T.astype(jnp.bfloat16)
            rows = pl.ds(pl.multiple_of((2 * b + o) * 32, 32), 32)
            for member in range(4):
                step = (member - x + 4) % 4
                sendbuf[step, rel, f, chunk, rows, :] = block[32 * member : 32 * member + 32]

    def columns_of(rel, f):
        return pl.ds(pl.multiple_of(((zs[rel] * 4 + x) * 2 + f) * EMB, EMB), EMB)

    def x_copy(rel, f, chunk, step):
        return pltpu.make_async_remote_copy(
            sendbuf.at[step, rel, f, chunk],
            base.at[rows_of(chunk), columns_of(rel, f)],
            x_send.at[step - 1, rel, f, chunk],
            x_recv.at[step - 1, rel, f, chunk],
            device_id=on_x(step),
            device_id_type=MESH,
        )

    def own_copy(rel, f, chunk):
        return pltpu.make_async_copy(
            sendbuf.at[0, rel, f, chunk],
            base.at[rows_of(chunk), columns_of(rel, f)],
            own_sem.at[rel, f, chunk],
        )

    def fill(rel, f, chunk):
        def one(b, carry):
            tile(rel, f, chunk, b)
            return carry

        lax.fori_loop(0, 4, one, 0, unroll=2)

    def give(rel, f, chunk):
        for step in (2, 1, 3):
            x_copy(rel, f, chunk, step).start()
        own_copy(rel, f, chunk).start()

    def pool(rel, f):
        turn(rel, f)
        for chunk in range(2):
            fill(rel, f, chunk)
            give(rel, f, chunk)

    def tell(stage):
        pl.semaphore_signal(pace.at[stage], inc=1, device_id=(t ^ 8, v), device_id_type=MESH)

    def hear(stage):
        pl.semaphore_wait(pace.at[stage], 1)

    def part_of(rel):
        return pl.ds(pl.multiple_of(zs[rel] * 1024, 1024), 1024)

    def arrived(rel, chunk):
        for f in range(2):
            for step in (1, 2, 3):
                x_copy(rel, f, chunk, step).wait_recv()
            own_copy(rel, f, chunk).wait()

    def lower(rel):
        arrived(rel, 0)
        arrived(rel, 1)
        part = part_of(rel)
        term = jnp.dot(base[:, part], down[part, :], preferred_element_type=jnp.float32)
        if rel == 0:
            acc[...] = term
        else:
            acc[...] += term

    own_tab.wait()
    turn(0, 0)
    fill(0, 0, 0)
    fill(0, 0, 1)
    pl.semaphore_wait(barrier, 21)
    for there in (1, 2):
        key_copy(there, 0).start()
        tab_copy(there, 0).start()
    give(0, 0, 0)
    give(0, 0, 1)
    pool(0, 1)
    for copy in weights:
        copy.start()

    def next_tables():
        hear(0)
        for there in (1, 2):
            key_copy(there, 1).start()
            tab_copy(there, 1).start()

    def next_forwards():
        hear(1)
        for f in range(2):
            key_copy(3, f).start()
        for there in (1, 2):
            forward(there, 0).start()

    for f, advance in ((0, next_tables), (1, next_forwards)):
        for there in (1, 2):
            tab_copy(there, f).wait_send()
        tell(f)
        advance()
        for rel in (1, 2):
            key_copy(rel, f).wait_recv()
            tab_copy(rel, f).wait_recv()
            pool(rel, f)
        if f == 0:
            for copy in weights:
                copy.wait()
            lower(0)
    for there in (1, 2):
        forward(there, 0).wait_send()
        forward(there, 1).start()
    for f in range(2):
        if f == 1:
            lower(1)
            lower(2)
        key_copy(3, f).wait_recv()
        for there in (1, 2):
            forward(there, f).wait_recv()
        pool(3, f)

    def out_copy(mask):
        return pltpu.make_async_remote_copy(
            outs.at[t ^ mask],
            gath.at[t],
            o_send.at[mask],
            o_recv.at[mask],
            device_id=(t ^ mask, v),
            device_id_type=MESH,
        )

    for chunk in range(2):
        r = rows_of(chunk)
        arrived(3, chunk)
        part = part_of(3)
        total = acc[r, :] + jnp.dot(
            base[r, part], down[part, :], preferred_element_type=jnp.float32
        )
        low[...] = total.astype(jnp.bfloat16)
        for n in range(16):
            c = slice(256 * n, 256 * n + 256)
            high = jnp.dot(low[...], up[:, c], preferred_element_type=jnp.float32) + bias_ref[:, c]
            b = base[r, c].astype(jnp.float32)
            cross[:, c] = (b * high + b).astype(jnp.bfloat16)
        value = jnp.dot(cross[...], proj[...], preferred_element_type=jnp.float32)
        value = (value + pbias_ref[...]).astype(jnp.bfloat16).reshape(8, 32, OUT)
        for i in range(8):
            outs[2 * i + half_of(chunk)] = value[i]
        for i in range(8):
            mask = 2 * i + chunk
            if mask:
                out_copy(mask).start()
    gath[t] = outs[t]
    for mask in range(1, 16):
        out_copy(mask).wait_recv()

    full = gath[...].reshape(512, OUT)
    gram = lax.dot_general(
        full, full, (((1,), (1,)), ((), ())), preferred_element_type=jnp.float32
    )
    same = (
        lax.broadcasted_iota(jnp.int32, (512, 512), 0) % 32
        == lax.broadcasted_iota(jnp.int32, (512, 512), 1) % 32
    )
    gram = jnp.where(same, gram, 0.0)
    fold = (
        lax.broadcasted_iota(jnp.int32, (512, 128), 0) // 32
        == lax.broadcasted_iota(jnp.int32, (512, 128), 1)
    ).astype(jnp.float32).astype(jnp.bfloat16)
    hi = gram.astype(jnp.bfloat16)
    rest = gram - hi.astype(jnp.float32)
    mid = rest.astype(jnp.bfloat16)
    folded = sum(jnp.dot(p, fold, preferred_element_type=jnp.float32) for p in (mid, hi))
    lane = lax.broadcasted_iota(jnp.int32, (32, 128), 1)
    result = jnp.zeros((32, 128), jnp.float32)
    start = 0
    for i in range(15):
        moved = pltpu.roll(folded[32 * i : 32 * i + 32], (start - i - 1) % 128, 1)
        result = jnp.where((lane >= start) & (lane < start + 15 - i), moved, result)
        start += 15 - i
    out_ref[...] = (result / jnp.sqrt(jnp.float32(OUT)))[:, :120]

    for f in range(2):
        for there in (1, 2, 3):
            key_copy(there, f).wait_send()
    for there in (1, 2):
        forward(there, 1).wait_send()
    for rel in range(4):
        for f in range(2):
            for chunk in range(2):
                for step in (1, 2, 3):
                    x_copy(rel, f, chunk, step).wait_send()
    for mask in range(1, 16):
        out_copy(mask).wait_send()


def local(bag_ids, bag_lengths, tables, cross_down, cross_up, cross_bias, proj_weight, proj_bias):
    bf, i32, f32 = jnp.bfloat16, jnp.int32, jnp.float32
    hbm = pl.BlockSpec(memory_space=pl.ANY)
    dma = pltpu.SemaphoreType.DMA
    return pl.pallas_call(
        kernel,
        out_shape=jax.ShapeDtypeStruct((32, 120), f32),
        in_specs=[hbm] * 8,
        out_specs=pl.BlockSpec(memory_space=pltpu.VMEM),
        scratch_shapes=[
            pltpu.VMEM((2, 4, 8192), i32),
            pltpu.VMEM((2, 8192), i32),
            pltpu.VMEM((1, 4096), f32),
            pltpu.VMEM((1, OUT), f32),
            pltpu.VMEM((4, 2, 2, 4, 8, 128), i32),
            pltpu.VMEM((3, 2, 2, 4, 8, 128), i32),
            pltpu.VMEM((1024, 128), bf),
            pltpu.VMEM((2, EMB, 1024), bf),
            pltpu.VMEM((4, 2, 1024, EMB), bf),
            pltpu.VMEM((4, 4, 2, 2, HALF, EMB), bf),
            pltpu.VMEM((512, 4096), bf),
            pltpu.VMEM((4096, 512), bf),
            pltpu.VMEM((512, 4096), bf),
            pltpu.VMEM((4096, 512), bf),
            pltpu.VMEM((512, 512), f32),
            pltpu.VMEM((HALF, 512), bf),
            pltpu.VMEM((HALF, 4096), bf),
            pltpu.VMEM((16, 32, OUT), bf),
            pltpu.VMEM((16, 32, OUT), bf),
            dma((8,)),
            dma((3, 2)),
            dma((3, 2)),
            dma((2, 2)),
            dma((2, 2)),
            dma((2, 2)),
            dma((2, 2)),
            dma((4, 2, 2)),
            pltpu.SemaphoreType.REGULAR((2,)),
            dma((3, 4, 2, 2)),
            dma((3, 4, 2, 2)),
            dma((16,)),
            dma((16,)),
        ],
        compiler_params=pltpu.CompilerParams(
            collective_id=0, has_side_effects=True, vmem_limit_bytes=60 << 20
        ),
    )(
        bag_ids[0].transpose(1, 2, 0),
        bag_lengths[0].transpose(1, 0),
        tables[0],
        cross_down[0, 0],
        cross_up[0, 0],
        cross_bias[0],
        proj_weight[0],
        proj_bias,
    )


def solution(mesh):
    placed = (
        P("tower", None, "dev", None),
        P("tower", None, "dev"),
        P("tower", "dev", None, None),
        P("tower", None, None, None),
        P("tower", None, None, None),
        P("tower", None, None),
        P("tower", None, None),
        P("tower", None),
    )
    return jax.shard_map(
        local, mesh=mesh, in_specs=placed, out_specs=P(("tower", "dev"), None), check_vma=False
    )
```

```python
import functools

import jax
import jax.numpy as jnp
from jax import lax
from jax.experimental import pallas as pl
from jax.experimental.pallas import tpu as pltpu
from jax.sharding import PartitionSpec as P

EMB = 128
OUT = 512
MESH = pl.DeviceIdType.MESH
HALF = 256


def kernel(
    ids_hbm,
    len_hbm,
    tab_hbm,
    down_hbm,
    up_hbm,
    bias_hbm,
    proj_hbm,
    pbias_hbm,
    out_ref,
    ids_ref,
    len_ref,
    bias_ref,
    pbias_ref,
    keys,
    keys_in,
    codes,
    turned,
    tab,
    sendbuf,
    base,
    down,
    up,
    proj,
    acc,
    low,
    cross,
    outs,
    gath,
    local_sem,
    k_send,
    k_recv,
    t_send,
    t_recv,
    f_send,
    f_recv,
    own_sem,
    pace,
    x_send,
    x_recv,
    o_send,
    o_recv,
):
    t = lax.axis_index("tower")
    v = lax.axis_index("dev")
    zh, x = v // 4, v % 4
    core, place = t % 2, t // 2
    right, left, opposite = (zh + 1) % 4, (zh + 3) % 4, (zh + 2) % 4
    zs = (zh, left, right, opposite)

    def on_z(z):
        return (t, z * 4 + x)

    def on_x(step):
        return (t, zh * 4 + (x + step) % 4)

    def half_of(chunk):
        return (core + chunk) % 2

    def rows_of(chunk):
        return pl.ds(pl.multiple_of(half_of(chunk) * HALF, HALF), HALF)

    barrier = pltpu.get_barrier_semaphore()
    for z in (right, left, opposite):
        pl.semaphore_signal(barrier, inc=1, device_id=on_z(z), device_id_type=MESH)
    for step in (1, 2, 3):
        pl.semaphore_signal(barrier, inc=1, device_id=on_x(step), device_id_type=MESH)
    for mask in range(1, 16):
        pl.semaphore_signal(barrier, inc=1, device_id=(t ^ mask, v), device_id_type=MESH)

    def fetch(k, src, dst):
        return pltpu.make_async_copy(src, dst, local_sem.at[k])

    first = [fetch(0, ids_hbm, ids_ref), fetch(1, len_hbm, len_ref)]
    own_tab = fetch(2, tab_hbm, tab.at[0])
    weights = [
        fetch(3, down_hbm, down),
        fetch(4, up_hbm, up),
        fetch(5, proj_hbm, proj),
        fetch(6, bias_hbm, bias_ref),
        fetch(7, pbias_hbm, pbias_ref),
    ]
    for copy in first:
        copy.start()
    own_tab.start()
    for copy in first:
        copy.wait()

    slot = lax.broadcasted_iota(jnp.int32, (4, 128), 0)

    def make_keys(n, carry):
        z, half, b = n % 4, (n // 4) % 2, n // 8
        for f in range(2):
            groups = []
            for o in range(2):
                start = (4 * b + 2 * o + half) * 512 + z * 128
                lanes = pl.ds(pl.multiple_of(start, 128), 128)
                row = ids_ref[f, :, lanes]
                live = slot < len_ref[f : f + 1, lanes]
                code = (128 + (row & 127)) << (row >> 7)
                groups.append(jnp.where(live, code, 0))
            keys[z, f, half, b] = jnp.concatenate(groups, axis=0)
        return carry

    lax.fori_loop(0, 32, make_keys, 0, unroll=2)

    def key_copy(there, f):
        z = (None, right, left, opposite)[there]
        return pltpu.make_async_remote_copy(
            keys.at[z, f],
            keys_in.at[there - 1, f],
            k_send.at[there - 1, f],
            k_recv.at[there - 1, f],
            device_id=on_z(z),
            device_id_type=MESH,
        )

    def tab_copy(there, f):
        return pltpu.make_async_remote_copy(
            tab_hbm.at[f],
            tab.at[there, f],
            t_send.at[there - 1, f],
            t_recv.at[there - 1, f],
            device_id=on_z((None, right, left)[there]),
            device_id_type=MESH,
        )

    def forward(there, f):
        rows = pl.ds((there - 1) * 512, 512)
        return pltpu.make_async_remote_copy(
            tab.at[there, f, rows],
            tab.at[3, f, rows],
            f_send.at[there - 1, f],
            f_recv.at[there - 1, f],
            device_id=on_z((None, right, left)[there]),
            device_id_type=MESH,
        )

    row_id = lax.broadcasted_iota(jnp.int32, (1024, 128), 0)
    codes[...] = ((128 + (row_id & 127)) << (row_id >> 7)).astype(jnp.float32).astype(jnp.bfloat16)
    lane_of = lax.broadcasted_iota(jnp.int32, (8, 128), 0) % 4

    def turn(rel, f):
        turned[f] = tab[rel, f].astype(jnp.float32).T.astype(jnp.bfloat16)

    def tile(rel, f, chunk, b):
        half = half_of(chunk)
        key = keys[zh, f, half, b] if rel == 0 else keys_in[rel - 1, f, half, b]
        key = key.astype(jnp.float32)
        weight = jnp.ones((8, 128), jnp.float32)
        for r in (1, 2, 3):
            other = jnp.where(lane_of >= r, pltpu.roll(key, r, 0), pltpu.roll(key, r + 4, 0))
            weight = weight + jnp.where(other == key, 1.0, 0.0)
        counts = []
        for o in range(2):
            count = jnp.zeros((1024, 128), jnp.bfloat16)
            for p in range(4 * o, 4 * o + 4):
                k, w = (
                    jnp.tile(jnp.broadcast_to(a[p : p + 1], (16, 128)).astype(jnp.bfloat16), (64, 1))
                    for a in (key, weight)
                )
                count = jnp.where(k == codes[...], w, count)
            counts.append(count)
        pooled = jnp.dot(
            turned[f], jnp.concatenate(counts, axis=1), preferred_element_type=jnp.float32
        )
        for o in range(2):
            block = pooled[:, 128 * o : 128 * o + 128].T.astype(jnp.bfloat16)
            rows = pl.ds(pl.multiple_of((2 * b + o) * 32, 32), 32)
            for member in range(4):
                step = (member - x + 4) % 4
                sendbuf[step, rel, f, chunk, rows, :] = block[32 * member : 32 * member + 32]

    def columns_of(rel, f):
        return pl.ds(pl.multiple_of(((zs[rel] * 4 + x) * 2 + f) * EMB, EMB), EMB)

    def x_copy(rel, f, chunk, step):
        return pltpu.make_async_remote_copy(
            sendbuf.at[step, rel, f, chunk],
            base.at[rows_of(chunk), columns_of(rel, f)],
            x_send.at[step - 1, rel, f, chunk],
            x_recv.at[step - 1, rel, f, chunk],
            device_id=on_x(step),
            device_id_type=MESH,
        )

    def own_copy(rel, f, chunk):
        return pltpu.make_async_copy(
            sendbuf.at[0, rel, f, chunk],
            base.at[rows_of(chunk), columns_of(rel, f)],
            own_sem.at[rel, f, chunk],
        )

    def fill(rel, f, chunk):
        def one(b, carry):
            tile(rel, f, chunk, b)
            return carry

        lax.fori_loop(0, 4, one, 0, unroll=2)

    def give(rel, f, chunk):
        for step in (2, 1, 3):
            x_copy(rel, f, chunk, step).start()
        own_copy(rel, f, chunk).start()

    def pool(rel, f):
        turn(rel, f)
        for chunk in range(2):
            fill(rel, f, chunk)
            give(rel, f, chunk)

    def tell(stage):
        pl.semaphore_signal(pace.at[stage], inc=1, device_id=(t ^ 8, v), device_id_type=MESH)

    def hear(stage):
        pl.semaphore_wait(pace.at[stage], 1)

    def part_of(rel):
        return pl.ds(pl.multiple_of(zs[rel] * 1024, 1024), 1024)

    def arrived(rel, chunk):
        for f in range(2):
            for step in (1, 2, 3):
                x_copy(rel, f, chunk, step).wait_recv()
            own_copy(rel, f, chunk).wait()

    def lower(rel):
        arrived(rel, 0)
        arrived(rel, 1)
        part = part_of(rel)
        term = jnp.dot(base[:, part], down[part, :], preferred_element_type=jnp.float32)
        if rel == 0:
            acc[...] = term
        else:
            acc[...] += term

    own_tab.wait()
    turn(0, 0)
    fill(0, 0, 0)
    pl.semaphore_wait(barrier, 21)
    for there in (1, 2):
        key_copy(there, 0).start()
        tab_copy(there, 0).start()
    give(0, 0, 0)
    fill(0, 0, 1)
    give(0, 0, 1)
    pool(0, 1)
    for copy in weights:
        copy.start()

    def next_tables():
        hear(0)
        for there in (1, 2):
            key_copy(there, 1).start()
            tab_copy(there, 1).start()
            key_copy(3, there - 1).start()

    def next_forwards():
        hear(1)
        for there in (1, 2):
            forward(there, 0).start()

    for f, advance in ((0, next_tables), (1, next_forwards)):
        for there in (1, 2):
            tab_copy(there, f).wait_send()
        tell(f)
        advance()
        for rel in (1, 2):
            key_copy(rel, f).wait_recv()
            tab_copy(rel, f).wait_recv()
            pool(rel, f)
        if f == 0:
            for copy in weights:
                copy.wait()
            lower(0)
    for there in (1, 2):
        forward(there, 0).wait_send()
        forward(there, 1).start()
    for f in range(2):
        if f == 1:
            lower(1)
            lower(2)
        key_copy(3, f).wait_recv()
        for there in (1, 2):
            forward(there, f).wait_recv()
        turn(3, f)
        fill(3, f, 0)
        give(3, f, 0)
        fill(3, f, 1)
        if f == 1:
            for step in (1, 2, 3):
                x_copy(3, 1, 0, step).wait_send()
        give(3, f, 1)

    def out_copy(mask):
        return pltpu.make_async_remote_copy(
            outs.at[t ^ mask],
            gath.at[t],
            o_send.at[mask],
            o_recv.at[mask],
            device_id=(t ^ mask, v),
            device_id_type=MESH,
        )

    for chunk in range(2):
        r = rows_of(chunk)
        arrived(3, chunk)
        part = part_of(3)
        total = acc[r, :] + jnp.dot(
            base[r, part], down[part, :], preferred_element_type=jnp.float32
        )
        low[...] = total.astype(jnp.bfloat16)
        for n in range(16):
            c = slice(256 * n, 256 * n + 256)
            high = jnp.dot(low[...], up[:, c], preferred_element_type=jnp.float32) + bias_ref[:, c]
            b = base[r, c].astype(jnp.float32)
            cross[:, c] = (b * high + b).astype(jnp.bfloat16)
        value = jnp.dot(cross[...], proj[...], preferred_element_type=jnp.float32)
        value = (value + pbias_ref[...]).astype(jnp.bfloat16).reshape(8, 32, OUT)
        for i in range(8):
            outs[2 * i + half_of(chunk)] = value[i]
        for i in reversed(range(8)):
            mask = 2 * i + chunk
            if mask:
                out_copy(mask).start()
    gath[t] = outs[t]
    for mask in range(1, 16):
        out_copy(mask).wait_recv()

    full = gath[...].reshape(512, OUT)
    gram = lax.dot_general(
        full, full, (((1,), (1,)), ((), ())), preferred_element_type=jnp.float32
    )
    same = (
        lax.broadcasted_iota(jnp.int32, (512, 512), 0) % 32
        == lax.broadcasted_iota(jnp.int32, (512, 512), 1) % 32
    )
    gram = jnp.where(same, gram, 0.0)
    fold = (
        lax.broadcasted_iota(jnp.int32, (512, 128), 0) // 32
        == lax.broadcasted_iota(jnp.int32, (512, 128), 1)
    ).astype(jnp.float32).astype(jnp.bfloat16)
    hi = gram.astype(jnp.bfloat16)
    rest = gram - hi.astype(jnp.float32)
    mid = rest.astype(jnp.bfloat16)
    folded = sum(jnp.dot(p, fold, preferred_element_type=jnp.float32) for p in (mid, hi))
    lane = lax.broadcasted_iota(jnp.int32, (32, 128), 1)
    result = jnp.zeros((32, 128), jnp.float32)
    start = 0
    for i in range(15):
        moved = pltpu.roll(folded[32 * i : 32 * i + 32], (start - i - 1) % 128, 1)
        result = jnp.where((lane >= start) & (lane < start + 15 - i), moved, result)
        start += 15 - i
    out_ref[...] = (result / jnp.sqrt(jnp.float32(OUT)))[:, :120]

    for f in range(2):
        for there in (1, 2, 3):
            key_copy(there, f).wait_send()
    for there in (1, 2):
        forward(there, 1).wait_send()
    for rel in range(4):
        for f in range(2):
            for chunk in range(2):
                if (rel, f, chunk) != (3, 1, 0):
                    for step in (1, 2, 3):
                        x_copy(rel, f, chunk, step).wait_send()
    for mask in range(1, 16):
        out_copy(mask).wait_send()


def local(bag_ids, bag_lengths, tables, cross_down, cross_up, cross_bias, proj_weight, proj_bias):
    bf, i32, f32 = jnp.bfloat16, jnp.int32, jnp.float32
    hbm = pl.BlockSpec(memory_space=pl.ANY)
    dma = pltpu.SemaphoreType.DMA
    return pl.pallas_call(
        kernel,
        out_shape=jax.ShapeDtypeStruct((32, 120), f32),
        in_specs=[hbm] * 8,
        out_specs=pl.BlockSpec(memory_space=pltpu.VMEM),
        scratch_shapes=[
            pltpu.VMEM((2, 4, 8192), i32),
            pltpu.VMEM((2, 8192), i32),
            pltpu.VMEM((1, 4096), f32),
            pltpu.VMEM((1, OUT), f32),
            pltpu.VMEM((4, 2, 2, 4, 8, 128), i32),
            pltpu.VMEM((3, 2, 2, 4, 8, 128), i32),
            pltpu.VMEM((1024, 128), bf),
            pltpu.VMEM((2, EMB, 1024), bf),
            pltpu.VMEM((4, 2, 1024, EMB), bf),
            pltpu.VMEM((4, 4, 2, 2, HALF, EMB), bf),
            pltpu.VMEM((512, 4096), bf),
            pltpu.VMEM((4096, 512), bf),
            pltpu.VMEM((512, 4096), bf),
            pltpu.VMEM((4096, 512), bf),
            pltpu.VMEM((512, 512), f32),
            pltpu.VMEM((HALF, 512), bf),
            pltpu.VMEM((HALF, 4096), bf),
            pltpu.VMEM((16, 32, OUT), bf),
            pltpu.VMEM((16, 32, OUT), bf),
            dma((8,)),
            dma((3, 2)),
            dma((3, 2)),
            dma((2, 2)),
            dma((2, 2)),
            dma((2, 2)),
            dma((2, 2)),
            dma((4, 2, 2)),
            pltpu.SemaphoreType.REGULAR((2,)),
            dma((3, 4, 2, 2)),
            dma((3, 4, 2, 2)),
            dma((16,)),
            dma((16,)),
        ],
        compiler_params=pltpu.CompilerParams(
            collective_id=0, has_side_effects=True, vmem_limit_bytes=60 << 20
        ),
    )(
        bag_ids[0].transpose(1, 2, 0),
        bag_lengths[0].transpose(1, 0),
        tables[0],
        cross_down[0, 0],
        cross_up[0, 0],
        cross_bias[0],
        proj_weight[0],
        proj_bias,
    )


def solution(mesh):
    placed = (
        P("tower", None, "dev", None),
        P("tower", None, "dev"),
        P("tower", "dev", None, None),
        P("tower", None, None, None),
        P("tower", None, None, None),
        P("tower", None, None),
        P("tower", None, None),
        P("tower", None),
    )
    return jax.shard_map(
        local, mesh=mesh, in_specs=placed, out_specs=P(("tower", "dev"), None), check_vma=False
    )
```

```python
import functools

import jax
import jax.numpy as jnp
from jax import lax
from jax.experimental import pallas as pl
from jax.experimental.pallas import tpu as pltpu
from jax.sharding import PartitionSpec as P

EMB = 128
OUT = 512
MESH = pl.DeviceIdType.MESH
HALF = 256


def kernel(
    ids_hbm,
    len_hbm,
    tab_hbm,
    down_hbm,
    up_hbm,
    bias_hbm,
    proj_hbm,
    pbias_hbm,
    out_ref,
    ids_ref,
    len_ref,
    bias_ref,
    pbias_ref,
    keys,
    keys_in,
    codes,
    turned,
    tab,
    sendbuf,
    base,
    down,
    up,
    proj,
    acc,
    low,
    cross,
    outs,
    gath,
    local_sem,
    k_send,
    k_recv,
    t_send,
    t_recv,
    f_send,
    f_recv,
    own_sem,
    pace,
    x_send,
    x_recv,
    o_send,
    o_recv,
):
    t = lax.axis_index("tower")
    v = lax.axis_index("dev")
    zh, x = v // 4, v % 4
    core, place = t % 2, t // 2
    right, left, opposite = (zh + 1) % 4, (zh + 3) % 4, (zh + 2) % 4
    zs = (zh, left, right, opposite)

    def on_z(z):
        return (t, z * 4 + x)

    def on_x(step):
        return (t, zh * 4 + (x + step) % 4)

    def half_of(chunk):
        return (core + chunk) % 2

    def rows_of(chunk):
        return pl.ds(pl.multiple_of(half_of(chunk) * HALF, HALF), HALF)

    barrier = pltpu.get_barrier_semaphore()
    for z in (right, left, opposite):
        pl.semaphore_signal(barrier, inc=1, device_id=on_z(z), device_id_type=MESH)
    for step in (1, 2, 3):
        pl.semaphore_signal(barrier, inc=1, device_id=on_x(step), device_id_type=MESH)
    for mask in range(1, 16):
        pl.semaphore_signal(barrier, inc=1, device_id=(t ^ mask, v), device_id_type=MESH)

    def fetch(k, src, dst):
        return pltpu.make_async_copy(src, dst, local_sem.at[k])

    first = [fetch(0, ids_hbm, ids_ref), fetch(1, len_hbm, len_ref)]
    own_tab = fetch(2, tab_hbm, tab.at[0])
    weights = [
        fetch(3, down_hbm, down),
        fetch(4, up_hbm, up),
        fetch(5, proj_hbm, proj),
        fetch(6, bias_hbm, bias_ref),
        fetch(7, pbias_hbm, pbias_ref),
    ]
    for copy in first:
        copy.start()
    own_tab.start()
    for copy in first:
        copy.wait()

    slot = lax.broadcasted_iota(jnp.int32, (4, 128), 0)

    def make_keys(n, carry):
        z, half, b = n % 4, (n // 4) % 2, n // 8
        for f in range(2):
            groups = []
            for o in range(2):
                start = (4 * b + 2 * o + half) * 512 + z * 128
                lanes = pl.ds(pl.multiple_of(start, 128), 128)
                row = ids_ref[f, :, lanes]
                live = slot < len_ref[f : f + 1, lanes]
                code = (128 + (row & 127)) << (row >> 7)
                groups.append(jnp.where(live, code, 0))
            keys[z, f, half, b] = jnp.concatenate(groups, axis=0)
        return carry

    lax.fori_loop(0, 32, make_keys, 0, unroll=2)

    def key_copy(there, f):
        z = (None, right, left, opposite)[there]
        return pltpu.make_async_remote_copy(
            keys.at[z, f],
            keys_in.at[there - 1, f],
            k_send.at[there - 1, f],
            k_recv.at[there - 1, f],
            device_id=on_z(z),
            device_id_type=MESH,
        )

    def tab_copy(there, f):
        return pltpu.make_async_remote_copy(
            tab_hbm.at[f],
            tab.at[there, f],
            t_send.at[there - 1, f],
            t_recv.at[there - 1, f],
            device_id=on_z((None, right, left)[there]),
            device_id_type=MESH,
        )

    def forward(there, f):
        rows = pl.ds((there - 1) * 512, 512)
        return pltpu.make_async_remote_copy(
            tab.at[there, f, rows],
            tab.at[3, f, rows],
            f_send.at[there - 1, f],
            f_recv.at[there - 1, f],
            device_id=on_z((None, right, left)[there]),
            device_id_type=MESH,
        )

    row_id = lax.broadcasted_iota(jnp.int32, (1024, 128), 0)
    codes[...] = ((128 + (row_id & 127)) << (row_id >> 7)).astype(jnp.float32).astype(jnp.bfloat16)
    lane_of = lax.broadcasted_iota(jnp.int32, (8, 128), 0) % 4

    def turn(rel, f):
        turned[f] = tab[rel, f].astype(jnp.float32).T.astype(jnp.bfloat16)

    def tile(rel, f, chunk, b):
        half = half_of(chunk)
        key = keys[zh, f, half, b] if rel == 0 else keys_in[rel - 1, f, half, b]
        key = key.astype(jnp.float32)
        weight = jnp.ones((8, 128), jnp.float32)
        for r in (1, 2, 3):
            other = jnp.where(lane_of >= r, pltpu.roll(key, r, 0), pltpu.roll(key, r + 4, 0))
            weight = weight + jnp.where(other == key, 1.0, 0.0)
        counts = []
        for o in range(2):
            count = jnp.zeros((1024, 128), jnp.bfloat16)
            for p in range(4 * o, 4 * o + 4):
                k, w = (
                    jnp.tile(jnp.broadcast_to(a[p : p + 1], (16, 128)).astype(jnp.bfloat16), (64, 1))
                    for a in (key, weight)
                )
                count = jnp.where(k == codes[...], w, count)
            counts.append(count)
        pooled = jnp.dot(
            turned[f], jnp.concatenate(counts, axis=1), preferred_element_type=jnp.float32
        )
        for o in range(2):
            block = pooled[:, 128 * o : 128 * o + 128].T.astype(jnp.bfloat16)
            rows = pl.ds(pl.multiple_of((2 * b + o) * 32, 32), 32)
            for member in range(4):
                step = (member - x + 4) % 4
                sendbuf[step, rel, f, chunk, rows, :] = block[32 * member : 32 * member + 32]

    def columns_of(rel, f):
        return pl.ds(pl.multiple_of(((zs[rel] * 4 + x) * 2 + f) * EMB, EMB), EMB)

    def x_copy(rel, f, chunk, step):
        return pltpu.make_async_remote_copy(
            sendbuf.at[step, rel, f, chunk],
            base.at[rows_of(chunk), columns_of(rel, f)],
            x_send.at[step - 1, rel, f, chunk],
            x_recv.at[step - 1, rel, f, chunk],
            device_id=on_x(step),
            device_id_type=MESH,
        )

    def own_copy(rel, f, chunk):
        return pltpu.make_async_copy(
            sendbuf.at[0, rel, f, chunk],
            base.at[rows_of(chunk), columns_of(rel, f)],
            own_sem.at[rel, f, chunk],
        )

    def fill(rel, f, chunk):
        def one(b, carry):
            tile(rel, f, chunk, b)
            return carry

        lax.fori_loop(0, 4, one, 0, unroll=2)

    def give(rel, f, chunk):
        for step in (2, 1, 3):
            x_copy(rel, f, chunk, step).start()
        own_copy(rel, f, chunk).start()

    def pool(rel, f):
        turn(rel, f)
        for chunk in range(2):
            fill(rel, f, chunk)
            give(rel, f, chunk)

    def tell(stage):
        pl.semaphore_signal(pace.at[stage], inc=1, device_id=(t ^ 8, v), device_id_type=MESH)

    def hear(stage):
        pl.semaphore_wait(pace.at[stage], 1)

    def part_of(rel):
        return pl.ds(pl.multiple_of(zs[rel] * 1024, 1024), 1024)

    def arrived(rel, chunk):
        for f in range(2):
            for step in (1, 2, 3):
                x_copy(rel, f, chunk, step).wait_recv()
            own_copy(rel, f, chunk).wait()

    def lower(rel):
        arrived(rel, 0)
        arrived(rel, 1)
        part = part_of(rel)
        term = jnp.dot(base[:, part], down[part, :], preferred_element_type=jnp.float32)
        if rel == 0:
            acc[...] = term
        else:
            acc[...] += term

    own_tab.wait()
    turn(0, 0)
    fill(0, 0, 0)
    pl.semaphore_wait(barrier, 21)
    for there in (1, 2):
        key_copy(there, 0).start()
        tab_copy(there, 0).start()
    give(0, 0, 0)
    fill(0, 0, 1)
    give(0, 0, 1)
    pool(0, 1)
    for copy in weights:
        copy.start()

    def next_tables():
        hear(0)
        for there in (1, 2):
            key_copy(there, 1).start()
            tab_copy(there, 1).start()
            key_copy(3, there - 1).start()

    def next_forwards():
        for there in (1, 2):
            forward(there, 0).start()

    for f, advance in ((0, next_tables), (1, next_forwards)):
        for there in (1, 2):
            tab_copy(there, f).wait_send()
        if f == 0:
            tell(f)
        advance()
        for rel in (1, 2):
            key_copy(rel, f).wait_recv()
            tab_copy(rel, f).wait_recv()
            pool(rel, f)
        if f == 0:
            for copy in weights:
                copy.wait()
            lower(0)
    for there in (1, 2):
        forward(there, 0).wait_send()
        forward(there, 1).start()
    for f in range(2):
        key_copy(3, f).wait_recv()
        for there in (1, 2):
            forward(there, f).wait_recv()
        turn(3, f)
        fill(3, f, 0)
        give(3, f, 0)
        fill(3, f, 1)
        if f == 1:
            lower(1)
            lower(2)
            for step in (1, 2, 3):
                x_copy(3, 1, 0, step).wait_send()
        give(3, f, 1)

    def out_copy(mask):
        return pltpu.make_async_remote_copy(
            outs.at[t ^ mask],
            gath.at[t],
            o_send.at[mask],
            o_recv.at[mask],
            device_id=(t ^ mask, v),
            device_id_type=MESH,
        )

    for chunk in range(2):
        r = rows_of(chunk)
        arrived(3, chunk)
        part = part_of(3)
        total = acc[r, :] + jnp.dot(
            base[r, part], down[part, :], preferred_element_type=jnp.float32
        )
        low[...] = total.astype(jnp.bfloat16)
        for n in range(16):
            c = slice(256 * n, 256 * n + 256)
            high = jnp.dot(low[...], up[:, c], preferred_element_type=jnp.float32) + bias_ref[:, c]
            b = base[r, c].astype(jnp.float32)
            cross[:, c] = (b * high + b).astype(jnp.bfloat16)
        value = jnp.dot(cross[...], proj[...], preferred_element_type=jnp.float32)
        value = (value + pbias_ref[...]).astype(jnp.bfloat16).reshape(8, 32, OUT)
        for i in range(8):
            outs[2 * i + half_of(chunk)] = value[i]
        for i in reversed(range(8)):
            mask = 2 * i + chunk
            if mask:
                out_copy(mask).start()
    gath[t] = outs[t]
    for mask in range(1, 16):
        out_copy(mask).wait_recv()

    full = gath[...].reshape(512, OUT)
    gram = lax.dot_general(
        full, full, (((1,), (1,)), ((), ())), preferred_element_type=jnp.float32
    )
    same = (
        lax.broadcasted_iota(jnp.int32, (512, 512), 0) % 32
        == lax.broadcasted_iota(jnp.int32, (512, 512), 1) % 32
    )
    gram = jnp.where(same, gram, 0.0)
    fold = (
        lax.broadcasted_iota(jnp.int32, (512, 128), 0) // 32
        == lax.broadcasted_iota(jnp.int32, (512, 128), 1)
    ).astype(jnp.float32).astype(jnp.bfloat16)
    hi = gram.astype(jnp.bfloat16)
    rest = gram - hi.astype(jnp.float32)
    mid = rest.astype(jnp.bfloat16)
    folded = sum(jnp.dot(p, fold, preferred_element_type=jnp.float32) for p in (mid, hi))
    lane = lax.broadcasted_iota(jnp.int32, (32, 128), 1)
    result = jnp.zeros((32, 128), jnp.float32)
    start = 0
    for i in range(15):
        moved = pltpu.roll(folded[32 * i : 32 * i + 32], (start - i - 1) % 128, 1)
        result = jnp.where((lane >= start) & (lane < start + 15 - i), moved, result)
        start += 15 - i
    out_ref[...] = (result / jnp.sqrt(jnp.float32(OUT)))[:, :120]

    for f in range(2):
        for there in (1, 2, 3):
            key_copy(there, f).wait_send()
    for there in (1, 2):
        forward(there, 1).wait_send()
    for rel in range(4):
        for f in range(2):
            for chunk in range(2):
                if (rel, f, chunk) != (3, 1, 0):
                    for step in (1, 2, 3):
                        x_copy(rel, f, chunk, step).wait_send()
    for mask in range(1, 16):
        out_copy(mask).wait_send()


def local(bag_ids, bag_lengths, tables, cross_down, cross_up, cross_bias, proj_weight, proj_bias):
    bf, i32, f32 = jnp.bfloat16, jnp.int32, jnp.float32
    hbm = pl.BlockSpec(memory_space=pl.ANY)
    dma = pltpu.SemaphoreType.DMA
    return pl.pallas_call(
        kernel,
        out_shape=jax.ShapeDtypeStruct((32, 120), f32),
        in_specs=[hbm] * 8,
        out_specs=pl.BlockSpec(memory_space=pltpu.VMEM),
        scratch_shapes=[
            pltpu.VMEM((2, 4, 8192), i32),
            pltpu.VMEM((2, 8192), i32),
            pltpu.VMEM((1, 4096), f32),
            pltpu.VMEM((1, OUT), f32),
            pltpu.VMEM((4, 2, 2, 4, 8, 128), i32),
            pltpu.VMEM((3, 2, 2, 4, 8, 128), i32),
            pltpu.VMEM((1024, 128), bf),
            pltpu.VMEM((2, EMB, 1024), bf),
            pltpu.VMEM((4, 2, 1024, EMB), bf),
            pltpu.VMEM((4, 4, 2, 2, HALF, EMB), bf),
            pltpu.VMEM((512, 4096), bf),
            pltpu.VMEM((4096, 512), bf),
            pltpu.VMEM((512, 4096), bf),
            pltpu.VMEM((4096, 512), bf),
            pltpu.VMEM((512, 512), f32),
            pltpu.VMEM((HALF, 512), bf),
            pltpu.VMEM((HALF, 4096), bf),
            pltpu.VMEM((16, 32, OUT), bf),
            pltpu.VMEM((16, 32, OUT), bf),
            dma((8,)),
            dma((3, 2)),
            dma((3, 2)),
            dma((2, 2)),
            dma((2, 2)),
            dma((2, 2)),
            dma((2, 2)),
            dma((4, 2, 2)),
            pltpu.SemaphoreType.REGULAR((1,)),
            dma((3, 4, 2, 2)),
            dma((3, 4, 2, 2)),
            dma((16,)),
            dma((16,)),
        ],
        compiler_params=pltpu.CompilerParams(
            collective_id=0, has_side_effects=True, vmem_limit_bytes=60 << 20
        ),
    )(
        bag_ids[0].transpose(1, 2, 0),
        bag_lengths[0].transpose(1, 0),
        tables[0],
        cross_down[0, 0],
        cross_up[0, 0],
        cross_bias[0],
        proj_weight[0],
        proj_bias,
    )


def solution(mesh):
    placed = (
        P("tower", None, "dev", None),
        P("tower", None, "dev"),
        P("tower", "dev", None, None),
        P("tower", None, None, None),
        P("tower", None, None, None),
        P("tower", None, None),
        P("tower", None, None),
        P("tower", None),
    )
    return jax.shard_map(
        local, mesh=mesh, in_specs=placed, out_specs=P(("tower", "dev"), None), check_vma=False
    )
```
